256 devices in a mesh: dp: 4 (over x), rows: 64 (over y, z, core).
Axes of the slice: x: 4, y: 4, z: 8, core: 2. Of those that a mesh axis runs over, the one named last changes fastest.
Arguments:
- grads: bfloat16 [4, 64, 1024, 1024], P('dp', None, 'rows'), may hold values from -6 to 6
- weight: bfloat16 [64, 1024, 1024], P(None, 'rows'), may hold values from -6 to 6
- basis: float32 [64, 1024, 256], P(None, 'rows'), may hold values from -6 to 6
- first_moment: float32 [256, 256, 1024], P('rows', None, 'dp'), may hold values from -6 to 6
- second_moment: float32 [256, 256, 1024], P('rows', None, 'dp'), may hold values from 0.5 to 4
- sketch: bfloat16 [1024, 256], replicated, may hold values from -6 to 6
- owner: int32 [64], replicated, may hold values from 0 to 63, as said below
- rank: int32 [64], replicated, may hold values from 128 to 256
Outputs:
- new_weight: bfloat16 [64, 1024, 1024], P(None, 'rows')
- new_basis: float32 [64, 1024, 256], P(None, 'rows')
- first_out: float32 [256, 256, 1024], P('rows', None, 'dp')
- second_out: float32 [256, 256, 1024], P('rows', None, 'dp')
The draws below stay inside these ranges and needn't reach their ends.
Inputs may be any that keep to these rules, and one draw needn't show every extreme that they name: No owner is named by more than 4 matrices, and some owner is named by exactly 4.
All inputs are finite; a program needn't handle non-finite values.
Results may differ from the reference program's by a relative error of at most 0.012.
Values may be sent and summed in bfloat16 or wider, within the bound.
A program may use at most 128 MiB of HBM per device.

```python
import jax
import jax.numpy as jnp
from jax import lax

MR = 1024
D = 1024
R = 256
CAP = 4
NMAT = 64
SLOTS = 256
GROUPS = 4
N_ROWS = 64


def draw_owner(key, part):
    key_first, key_second, key_third = jax.random.split(key, 3)
    slot_ids = jnp.arange(SLOTS, dtype=jnp.int32)
    chosen = jax.random.randint(key_first, (), 0, N_ROWS, dtype=jnp.int32)
    noise = jax.random.randint(key_second, (SLOTS,), 0, 1 << 20, dtype=jnp.int32)
    scores = noise * SLOTS + slot_ids
    scores = jnp.where(slot_ids // CAP == chosen, -1 - slot_ids, scores)
    ordering = jnp.argsort(scores, stable=True)
    picked = ordering[:NMAT]
    shuffle = jax.random.permutation(key_third, NMAT)
    return (picked[shuffle] // CAP).astype(jnp.int32)


def with_ends(result, stream_key, smallest, high):
    spot = [jax.random.randint(jax.random.fold_in(stream_key, axis), (), 0, length) for axis, length in enumerate(result.shape)]
    longest = result.shape.index(max(result.shape))
    next_to = spot[:longest] + [(spot[longest] + 1) % result.shape[longest]] + spot[longest + 1:]
    return result.at[tuple(spot)].set(smallest).at[tuple(next_to)].set(high)


def block_scale(stream_key, shape, cuts, low, largest):
    gain = 1.0
    for axis_at, blocks in cuts:
        steps = jax.random.uniform(jax.random.fold_in(jax.random.fold_in(stream_key, 6), axis_at), (blocks,), jnp.float32, low / len(cuts), largest / len(cuts))
        gain = gain * jnp.repeat(jnp.exp(steps), shape[axis_at] // blocks).reshape((-1,) + (1,) * (len(shape) - 1 - axis_at))
    return gain


def gaussian(rng, shape, spread, reach, pieces=(), kind=jnp.bfloat16):
    entries = spread * jax.random.normal(rng, shape, jnp.float32)
    if pieces:
        entries = entries * block_scale(rng, shape, pieces, -0.22, 0.18)
    return jnp.clip(entries, -reach, reach).astype(kind)


def setup_inputs(seed: int = 0) -> dict:
    keys = jax.random.split(jax.random.key(seed), 9)
    grads = gaussian(keys[0], (GROUPS, NMAT, MR, D), 1.0, 6.0, ((0, 4), (2, 64)))
    weight = gaussian(keys[1], (NMAT, MR, D), 1.0, 6.0, ((1, 64),))
    basis = gaussian(keys[2], (NMAT, MR, R), 1.0, 6.0, ((1, 64),), jnp.float32)
    first_moment = gaussian(keys[3], (SLOTS, R, D), 1.0, 6.0, ((0, 64), (2, 4)), jnp.float32)
    second_moment = jnp.clip(0.5 + 3.5 * jax.random.uniform(keys[4], (SLOTS, R, D), jnp.float32) ** block_scale(keys[4], (SLOTS, R, D), ((0, 64), (2, 4)), -0.2, 0.2), 0.5, 4.0)
    sketch = gaussian(keys[5], (D, R), 1.0, 6.0)
    owner = draw_owner(jax.random.fold_in(keys[8], 71), 0)
    rank = with_ends(jax.random.randint(keys[7], (NMAT,), R // 2, R + 1), jax.random.fold_in(keys[7], 1), R // 2, R).astype(jnp.int32)
    return dict(grads=grads, weight=weight, basis=basis, first_moment=first_moment, second_moment=second_moment, sketch=sketch, owner=owner, rank=rank)


beta_one = 0.9
beta_two = 0.95
bias_one = 1.0 - 0.9 ** 10
bias_two = 1.0 - 0.95 ** 10
step_size = 0.5
epsilon = 1e-08

def slot_of(owner):
    same = owner[:, None] == owner[None, :]
    places = jnp.arange(owner.shape[0], dtype=jnp.int32)
    earlier = places[None, :] < places[:, None]
    within = lax.optimization_barrier(jnp.sum((same & earlier).astype(jnp.int32), axis=1))
    return (owner * CAP + within).astype(jnp.int32)

def refresh(gradient, sketch, root):
    sample = jnp.dot(gradient.astype(jnp.float32), sketch.astype(jnp.float32), preferred_element_type=jnp.float32)
    gram = jnp.dot(sample.T, sample, precision=lax.Precision.HIGHEST)
    lower = jnp.linalg.cholesky(gram)
    solved = lax.linalg.triangular_solve(lower, sample, left_side=False, lower=True, transpose_a=True)
    return solved * root

def reference(grads, weight, basis, first_moment, second_moment, sketch, owner, rank):
    root = float(MR) ** 0.5
    inverse_root = float(MR) ** (-0.5)
    gradient = lax.optimization_barrier(jnp.sum(grads.astype(jnp.float32), axis=0)).astype(jnp.bfloat16)
    slots = slot_of(owner)
    rank_rows = jnp.arange(R, dtype=jnp.int32)

    def single(index):
        grad_one = gradient[index]
        basis_one = basis[index]
        slot_one = slots[index]
        grad_wide = lax.optimization_barrier(grad_one).astype(jnp.float32)
        projected = jnp.dot(basis_one.T, grad_wide, precision=lax.Precision.HIGHEST) * inverse_root
        first_new = beta_one * first_moment[slot_one] + (1.0 - beta_one) * projected
        second_new = beta_two * second_moment[slot_one] + (1.0 - beta_two) * projected * projected
        keeping = (rank_rows < rank[index]).astype(jnp.float32)[:, None]
        update = keeping * (first_new / bias_one) / (jnp.sqrt(second_new / bias_two) + epsilon)
        delta = (jnp.dot(basis_one, update, precision=lax.Precision.HIGHEST) * inverse_root).astype(jnp.bfloat16)
        delta = lax.optimization_barrier(delta)
        weight_new = (weight[index].astype(jnp.float32) - step_size * delta.astype(jnp.float32)).astype(jnp.bfloat16)
        return (weight_new, refresh(grad_one, sketch, root), first_new, second_new)
    new_weight, new_basis, first_new, second_new = lax.map(single, jnp.arange(NMAT, dtype=jnp.int32))
    first_out = jnp.zeros((SLOTS, R, D), jnp.float32).at[slots].set(first_new)
    second_out = jnp.zeros((SLOTS, R, D), jnp.float32).at[slots].set(second_new)
    return (new_weight, new_basis, first_out, second_out)
```

```python
import jax
import jax.numpy as jnp
from jax import lax
from jax.experimental import pallas as pl
from jax.experimental.pallas import tpu as pltpu
from jax.sharding import PartitionSpec as P

beta_one = 0.9
beta_two = 0.95
bias_one = 1.0 - 0.9**10
bias_two = 1.0 - 0.95**10
step_size = 0.5
epsilon = 1e-08

PANEL = 32


def slot_of(owner, capacity):
    same = owner[:, None] == owner[None, :]
    places = jnp.arange(owner.shape[0], dtype=jnp.int32)
    earlier = places[None, :] < places[:, None]
    within = jnp.sum((same & earlier).astype(jnp.int32), axis=1)
    return owner * capacity + within


def inverse_factor_kernel(gram_ref, out_ref, work_ref):
    size = gram_ref.shape[0]
    wide = 2 * size
    work_ref[:, :size] = gram_ref[...]
    row = lax.broadcasted_iota(jnp.int32, (size, size), 0)
    col = lax.broadcasted_iota(jnp.int32, (size, size), 1)
    work_ref[:, size:] = jnp.where(row == col, 1.0, 0.0)
    lane = lax.broadcasted_iota(jnp.int32, (PANEL, 128), 1)
    below = lax.broadcasted_iota(jnp.int32, (PANEL, 128), 0)
    unit = jnp.where(lane == below + PANEL, 1.0, 0.0)
    wide_lane = lax.broadcasted_iota(jnp.int32, (PANEL, size), 1)

    def panel(step, carry):
        head = work_ref[:PANEL, :]
        aug = jnp.where(lane < PANEL, head[:, :128], unit)
        scale = jnp.zeros((PANEL, 128), jnp.float32)
        for j in range(PANEL):
            pivot_row = aug[j : j + 1, :]
            column = jnp.broadcast_to(aug[:, j : j + 1], (PANEL, 128))
            pivot = column[j : j + 1, :]
            factor = jnp.where(below > j, column / pivot, 0.0)
            scale = jnp.where(below == j, lax.rsqrt(pivot), scale)
            aug = aug - factor * pivot_row
        inverse = (aug * scale)[:, PANEL : 2 * PANEL]
        solved = jnp.dot(
            inverse, head, precision=lax.Precision.HIGHEST, preferred_element_type=jnp.float32
        )
        rolled = pltpu.roll(solved, lax.rem(step * PANEL + size, wide), axis=1)
        out_ref[pl.ds(pl.multiple_of(step * PANEL, PANEL), PANEL), :] = rolled[:, :size]
        left = jnp.where(wide_lane < size - step * PANEL, solved[:, :size], 0.0)
        change = lax.dot_general(
            left,
            solved,
            (((0,), (0,)), ((), ())),
            precision=lax.Precision.HIGHEST,
            preferred_element_type=jnp.float32,
        )
        fresh = work_ref[PANEL:, :] - change[PANEL:, :]
        work_ref[: size - PANEL, :] = pltpu.roll(fresh, wide - PANEL, axis=1)
        return carry

    lax.fori_loop(0, size // PANEL, panel, 0)


def inverse_factor(gram):
    size = gram.shape[0]
    return pl.pallas_call(
        inverse_factor_kernel,
        out_shape=jax.ShapeDtypeStruct((size, size), jnp.float32),
        in_specs=[pl.BlockSpec(memory_space=pltpu.VMEM)],
        out_specs=pl.BlockSpec(memory_space=pltpu.VMEM),
        scratch_shapes=[pltpu.VMEM((size, 2 * size), jnp.float32)],
        cost_estimate=pl.CostEstimate(
            flops=20000000000, bytes_accessed=8 * size * size, transcendentals=0
        ),
        name="inverse_factor",
    )(gram)


def pick_kernel(index_ref, data_ref, out_ref):
    count = out_ref.shape[0]

    def one(i, carry):
        place = index_ref[i]
        block = data_ref[jnp.maximum(place, 0)]
        out_ref[i] = jnp.where(place >= 0, block, jnp.zeros_like(block))
        return carry

    lax.fori_loop(0, count, one, 0, unroll=4)


def pick(index, data):
    return pl.pallas_call(
        pick_kernel,
        out_shape=jax.ShapeDtypeStruct((index.shape[0],) + data.shape[1:], data.dtype),
        in_specs=[
            pl.BlockSpec(memory_space=pltpu.SMEM),
            pl.BlockSpec(memory_space=pltpu.VMEM),
        ],
        out_specs=pl.BlockSpec(memory_space=pltpu.VMEM),
        name="pick",
    )(index, data)


def to_chunks(data):
    rows, cols = data.shape[-2:]
    lead = data.shape[:-2]
    n = len(lead)
    tiles = data.reshape(lead + (rows // 8, 8, cols // 128, 128))
    tiles = jnp.transpose(tiles, tuple(range(n)) + (n, n + 2, n + 1, n + 3))
    return tiles.reshape(lead + (rows // 8 * (cols // 128), 8, 128))


def from_chunks(data, rows, cols):
    lead = data.shape[:-3]
    n = len(lead)
    tiles = data.reshape(lead + (rows // 8, cols // 128, 8, 128))
    tiles = jnp.transpose(tiles, tuple(range(n)) + (n, n + 2, n + 1, n + 3))
    return tiles.reshape(lead + (rows, cols))


def exchange(data, axis=0):
    return lax.all_to_all(data, "rows", split_axis=axis, concat_axis=axis, tiled=True)


def per_device(grads, weight, basis, first_moment, second_moment, sketch, owner, rank):
    owners = lax.axis_size("rows")
    groups = lax.axis_size("dp")
    here = lax.axis_index("rows")
    capacity, rank_full, quarter = first_moment.shape
    count, shard, width = weight.shape
    total_rows = shard * owners
    root = float(total_rows) ** 0.5
    inverse_root = float(total_rows) ** (-0.5)
    slots = slot_of(owner, capacity)
    column = slots % capacity * owners + slots // capacity
    column_ids = jnp.arange(capacity * owners, dtype=jnp.int32)
    hit = column[:, None] == column_ids[None, :]
    matrix_ids = jnp.arange(count, dtype=jnp.int32)
    source = jnp.max(jnp.where(hit, matrix_ids[:, None], -1), axis=0)

    parts = jnp.transpose(grads[0].reshape(count, shard, groups, quarter), (2, 0, 1, 3))
    parts = lax.all_to_all(parts, "dp", split_axis=0, concat_axis=0, tiled=True)
    mine = jnp.sum(parts.astype(jnp.float32), axis=0).astype(jnp.bfloat16)

    old_basis = exchange(basis.astype(jnp.bfloat16)).reshape(total_rows, rank_full)

    moments = jnp.stack(
        [
            to_chunks(first_moment.astype(jnp.bfloat16)),
            to_chunks(second_moment.astype(jnp.bfloat16)),
        ],
        axis=2,
    )
    moments = exchange(moments, axis=1)
    moments = pick(column, moments.reshape(capacity * owners, 16, 128))
    moments = exchange(moments).reshape(owners, 2, 8, 128)
    first_old = from_chunks(moments[:, 0], rank_full, quarter).astype(jnp.float32)
    second_old = from_chunks(moments[:, 1], rank_full, quarter).astype(jnp.float32)

    own = exchange(mine).reshape(total_rows, quarter)
    whole = lax.all_gather(own, "dp", axis=1, tiled=True)

    projected = (
        lax.dot_general(
            old_basis, own, (((0,), (0,)), ((), ())), preferred_element_type=jnp.float32
        )
        * inverse_root
    )
    first_new = beta_one * first_old + (1.0 - beta_one) * projected
    second_new = beta_two * second_old + (1.0 - beta_two) * projected * projected
    my_rank = lax.dynamic_index_in_dim(rank, here, keepdims=False)
    keeping = (jnp.arange(rank_full, dtype=jnp.int32) < my_rank).astype(jnp.float32)[:, None]
    update = keeping * (first_new / bias_one) / (jnp.sqrt(second_new / bias_two) + epsilon)
    delta = (
        jnp.dot(old_basis, update.astype(jnp.bfloat16), preferred_element_type=jnp.float32)
        * inverse_root
    ).astype(jnp.bfloat16)
    back_delta = exchange(delta.reshape(owners, shard, quarter))
    full_delta = lax.all_gather(back_delta, "dp", axis=2, tiled=True)
    new_weight = (weight.astype(jnp.float32) - step_size * full_delta.astype(jnp.float32)).astype(
        jnp.bfloat16
    )

    spread = exchange(to_chunks(projected.astype(jnp.bfloat16)))
    spread = pick(source, spread).reshape(capacity, owners, 8, 128)
    spread = exchange(spread, axis=1)
    here_projected = from_chunks(spread, rank_full, quarter).astype(jnp.float32)
    matched = slots[:, None] == (here * capacity + jnp.arange(capacity, dtype=jnp.int32))[None, :]
    valid = jnp.any(matched, axis=0)[:, None, None]
    first_out = jnp.where(
        valid, beta_one * first_moment + (1.0 - beta_one) * here_projected, 0.0
    )
    second_out = jnp.where(
        valid,
        beta_two * second_moment + (1.0 - beta_two) * here_projected * here_projected,
        0.0,
    )

    sample = jnp.dot(whole, sketch, preferred_element_type=jnp.float32)
    gram = lax.dot_general(
        sample, sample, (((0,), (0,)), ((), ())), precision=lax.Precision.HIGHEST
    )
    inverse = inverse_factor(gram)
    solved = lax.dot_general(
        sample, inverse, (((1,), (1,)), ((), ())), precision=lax.Precision.HIGHEST
    )
    fresh = (solved * root).astype(jnp.bfloat16).reshape(owners, shard, rank_full)
    new_basis = exchange(fresh).astype(jnp.float32)
    return (new_weight, new_basis, first_out, second_out)


def solution(mesh):
    in_specs = (
        P("dp", None, "rows", None),
        P(None, "rows", None),
        P(None, "rows", None),
        P("rows", None, "dp"),
        P("rows", None, "dp"),
        P(),
        P(),
        P(),
    )
    out_specs = (
        P(None, "rows", None),
        P(None, "rows", None),
        P("rows", None, "dp"),
        P("rows", None, "dp"),
    )
    return jax.shard_map(
        per_device, mesh=mesh, in_specs=in_specs, out_specs=out_specs, check_vma=False
    )
```

```python
import jax
import jax.numpy as jnp
from jax import lax
from jax.experimental import pallas as pl
from jax.experimental.pallas import tpu as pltpu
from jax.sharding import PartitionSpec as P

beta_one = 0.9
beta_two = 0.95
bias_one = 1.0 - 0.9**10
bias_two = 1.0 - 0.95**10
step_size = 0.5
epsilon = 1e-08

PANEL = 32


def slot_of(owner, capacity):
    same = owner[:, None] == owner[None, :]
    places = jnp.arange(owner.shape[0], dtype=jnp.int32)
    earlier = places[None, :] < places[:, None]
    within = jnp.sum((same & earlier).astype(jnp.int32), axis=1)
    return owner * capacity + within


def inverse_factor_kernel(gram_ref, out_ref, work_ref):
    size = gram_ref.shape[0]
    wide = 2 * size
    work_ref[:, :size] = gram_ref[...]
    row = lax.broadcasted_iota(jnp.int32, (size, size), 0)
    col = lax.broadcasted_iota(jnp.int32, (size, size), 1)
    work_ref[:, size:] = jnp.where(row == col, 1.0, 0.0)
    lane = lax.broadcasted_iota(jnp.int32, (PANEL, 128), 1)
    below = lax.broadcasted_iota(jnp.int32, (PANEL, 128), 0)
    unit = jnp.where(lane == below + PANEL, 1.0, 0.0)
    wide_lane = lax.broadcasted_iota(jnp.int32, (PANEL, size), 1)

    def panel(step, carry):
        head = work_ref[:PANEL, :]
        aug = jnp.where(lane < PANEL, head[:, :128], unit)
        scale = jnp.zeros((PANEL, 128), jnp.float32)
        for j in range(PANEL):
            pivot_row = aug[j : j + 1, :]
            column = jnp.broadcast_to(aug[:, j : j + 1], (PANEL, 128))
            pivot = column[j : j + 1, :]
            factor = jnp.where(below > j, column / pivot, 0.0)
            scale = jnp.where(below == j, lax.rsqrt(pivot), scale)
            aug = aug - factor * pivot_row
        inverse = (aug * scale)[:, PANEL : 2 * PANEL]
        solved = jnp.dot(
            inverse, head, precision=lax.Precision.HIGHEST, preferred_element_type=jnp.float32
        )
        rolled = pltpu.roll(solved, lax.rem(step * PANEL + size, wide), axis=1)
        out_ref[pl.ds(pl.multiple_of(step * PANEL, PANEL), PANEL), :] = rolled[:, :size]
        left = jnp.where(wide_lane < size - step * PANEL, solved[:, :size], 0.0)
        change = lax.dot_general(
            left,
            solved,
            (((0,), (0,)), ((), ())),
            precision=lax.Precision.HIGHEST,
            preferred_element_type=jnp.float32,
        )
        fresh = work_ref[PANEL:, :] - change[PANEL:, :]
        work_ref[: size - PANEL, :] = pltpu.roll(fresh, wide - PANEL, axis=1)
        return carry

    lax.fori_loop(0, size // PANEL, panel, 0)


def inverse_factor(gram):
    size = gram.shape[0]
    return pl.pallas_call(
        inverse_factor_kernel,
        out_shape=jax.ShapeDtypeStruct((size, size), jnp.float32),
        in_specs=[pl.BlockSpec(memory_space=pltpu.VMEM)],
        out_specs=pl.BlockSpec(memory_space=pltpu.VMEM),
        scratch_shapes=[pltpu.VMEM((size, 2 * size), jnp.float32)],
        cost_estimate=pl.CostEstimate(
            flops=20000000000, bytes_accessed=8 * size * size, transcendentals=0
        ),
        name="inverse_factor",
    )(gram)


def pick_kernel(index_ref, data_ref, out_ref):
    count = out_ref.shape[0]

    def one(i, carry):
        place = index_ref[i]
        block = data_ref[jnp.maximum(place, 0)]
        out_ref[i] = jnp.where(place >= 0, block, jnp.zeros_like(block))
        return carry

    lax.fori_loop(0, count, one, 0, unroll=4)


def pick(index, data):
    return pl.pallas_call(
        pick_kernel,
        out_shape=jax.ShapeDtypeStruct((index.shape[0],) + data.shape[1:], data.dtype),
        in_specs=[
            pl.BlockSpec(memory_space=pltpu.SMEM),
            pl.BlockSpec(memory_space=pltpu.VMEM),
        ],
        out_specs=pl.BlockSpec(memory_space=pltpu.VMEM),
        name="pick",
    )(index, data)


def to_chunks(data):
    rows, cols = data.shape[-2:]
    lead = data.shape[:-2]
    n = len(lead)
    tiles = data.reshape(lead + (rows // 8, 8, cols // 128, 128))
    tiles = jnp.transpose(tiles, tuple(range(n)) + (n, n + 2, n + 1, n + 3))
    return tiles.reshape(lead + (rows // 8 * (cols // 128), 8, 128))


def from_chunks(data, rows, cols):
    lead = data.shape[:-3]
    n = len(lead)
    tiles = data.reshape(lead + (rows // 8, cols // 128, 8, 128))
    tiles = jnp.transpose(tiles, tuple(range(n)) + (n, n + 2, n + 1, n + 3))
    return tiles.reshape(lead + (rows, cols))


def exchange(data, axis=0):
    return lax.all_to_all(data, "rows", split_axis=axis, concat_axis=axis, tiled=True)


def per_device(grads, weight, basis, first_moment, second_moment, sketch, owner, rank):
    owners = lax.axis_size("rows")
    groups = lax.axis_size("dp")
    here = lax.axis_index("rows")
    capacity, rank_full, quarter = first_moment.shape
    count, shard, width = weight.shape
    total_rows = shard * owners
    root = float(total_rows) ** 0.5
    inverse_root = float(total_rows) ** (-0.5)
    slots = slot_of(owner, capacity)
    slot_ids = jnp.arange(capacity * owners, dtype=jnp.int32)
    hit = slots[:, None] == slot_ids[None, :]
    matrix_ids = jnp.arange(count, dtype=jnp.int32)
    source = jnp.max(jnp.where(hit, matrix_ids[:, None], -1), axis=0)
    pieces = shard * quarter // 1024

    moments = jnp.stack(
        [
            to_chunks(first_moment.astype(jnp.bfloat16)),
            to_chunks(second_moment.astype(jnp.bfloat16)),
        ],
        axis=2,
    )
    moments = jnp.transpose(moments, (1, 0, 2, 3, 4)).reshape(owners, 2 * capacity, 8, 128)
    first_trip = jnp.concatenate([moments, to_chunks(basis.astype(jnp.bfloat16))], axis=1)
    first_trip = exchange(first_trip)
    moments = first_trip[:, : 2 * capacity].reshape(owners * capacity, 16, 128)
    old_basis = from_chunks(first_trip[:, 2 * capacity :], shard, rank_full)
    old_basis = old_basis.reshape(total_rows, rank_full)
    moments = pick(slots, moments).reshape(count, 2, 8, 128)

    parts = jnp.transpose(grads[0].reshape(count, shard, groups, quarter), (2, 0, 1, 3))
    parts = lax.all_to_all(parts, "dp", split_axis=0, concat_axis=0, tiled=True)
    mine = jnp.sum(parts.astype(jnp.float32), axis=0).astype(jnp.bfloat16)

    second_trip = exchange(jnp.concatenate([to_chunks(mine), moments], axis=1))
    own = from_chunks(second_trip[:, :pieces], shard, quarter).reshape(total_rows, quarter)
    first_old = from_chunks(second_trip[:, pieces], rank_full, quarter).astype(jnp.float32)
    second_old = from_chunks(second_trip[:, pieces + 1], rank_full, quarter).astype(jnp.float32)
    whole = lax.all_gather(own, "dp", axis=1, tiled=True)

    projected = (
        lax.dot_general(
            old_basis, own, (((0,), (0,)), ((), ())), preferred_element_type=jnp.float32
        )
        * inverse_root
    )
    first_new = beta_one * first_old + (1.0 - beta_one) * projected
    second_new = beta_two * second_old + (1.0 - beta_two) * projected * projected
    my_rank = lax.dynamic_index_in_dim(rank, here, keepdims=False)
    keeping = (jnp.arange(rank_full, dtype=jnp.int32) < my_rank).astype(jnp.float32)[:, None]
    update = keeping * (first_new / bias_one) / (jnp.sqrt(second_new / bias_two) + epsilon)
    delta = (
        jnp.dot(old_basis, update.astype(jnp.bfloat16), preferred_element_type=jnp.float32)
        * inverse_root
    ).astype(jnp.bfloat16)

    third_trip = exchange(
        jnp.concatenate(
            [
                to_chunks(delta.reshape(owners, shard, quarter)),
                to_chunks(projected.astype(jnp.bfloat16))[:, None],
            ],
            axis=1,
        )
    )
    back_delta = from_chunks(third_trip[:, :pieces], shard, quarter)
    full_delta = lax.all_gather(back_delta, "dp", axis=2, tiled=True)
    new_weight = (weight.astype(jnp.float32) - step_size * full_delta.astype(jnp.float32)).astype(
        jnp.bfloat16
    )

    spread = pick(source, third_trip[:, pieces]).reshape(owners, capacity, 8, 128)
    spread = jnp.transpose(exchange(spread), (1, 0, 2, 3))
    here_projected = from_chunks(spread, rank_full, quarter).astype(jnp.float32)
    matched = slots[:, None] == (here * capacity + jnp.arange(capacity, dtype=jnp.int32))[None, :]
    valid = jnp.any(matched, axis=0)[:, None, None]
    first_out = jnp.where(
        valid, beta_one * first_moment + (1.0 - beta_one) * here_projected, 0.0
    )
    second_out = jnp.where(
        valid,
        beta_two * second_moment + (1.0 - beta_two) * here_projected * here_projected,
        0.0,
    )

    sample = jnp.dot(whole, sketch, preferred_element_type=jnp.float32)
    gram = lax.dot_general(
        sample, sample, (((0,), (0,)), ((), ())), precision=lax.Precision.HIGHEST
    )
    inverse = inverse_factor(gram)
    solved = lax.dot_general(
        sample, inverse, (((1,), (1,)), ((), ())), precision=lax.Precision.HIGHEST
    )
    fresh = (solved * root).astype(jnp.bfloat16).reshape(owners, shard, rank_full)
    new_basis = exchange(fresh).astype(jnp.float32)
    return (new_weight, new_basis, first_out, second_out)


def solution(mesh):
    in_specs = (
        P("dp", None, "rows", None),
        P(None, "rows", None),
        P(None, "rows", None),
        P("rows", None, "dp"),
        P("rows", None, "dp"),
        P(),
        P(),
        P(),
    )
    out_specs = (
        P(None, "rows", None),
        P(None, "rows", None),
        P("rows", None, "dp"),
        P("rows", None, "dp"),
    )
    return jax.shard_map(
        per_device, mesh=mesh, in_specs=in_specs, out_specs=out_specs, check_vma=False
    )
```

```python
import jax
import jax.numpy as jnp
from jax import lax
from jax.experimental import pallas as pl
from jax.experimental.pallas import tpu as pltpu
from jax.sharding import PartitionSpec as P

beta_one = 0.9
beta_two = 0.95
bias_one = 1.0 - 0.9**10
bias_two = 1.0 - 0.95**10
step_size = 0.5
epsilon = 1e-08

PANEL = 64
BLOCK = 8


def slot_of(owner, capacity):
    same = owner[:, None] == owner[None, :]
    places = jnp.arange(owner.shape[0], dtype=jnp.int32)
    earlier = places[None, :] < places[:, None]
    within = jnp.sum((same & earlier).astype(jnp.int32), axis=1)
    return owner * capacity + within


def inverse_factor_kernel(gram_ref, out_ref, work_ref):
    size = gram_ref.shape[0]
    wide = 2 * size
    work_ref[:, :size] = gram_ref[...]
    row = lax.broadcasted_iota(jnp.int32, (size, size), 0)
    col = lax.broadcasted_iota(jnp.int32, (size, size), 1)
    work_ref[:, size:] = jnp.where(row == col, 1.0, 0.0)
    lane = lax.broadcasted_iota(jnp.int32, (8, 128), 1)
    below = lax.broadcasted_iota(jnp.int32, (8, 128), 0)
    wide_lane = lax.broadcasted_iota(jnp.int32, (PANEL, size), 1)
    tiles = PANEL // 8

    def spread(line):
        return jnp.broadcast_to(line, (8, 128))

    def panel(step, carry):
        head = work_ref[:PANEL, :]
        aug = []
        for t in range(tiles):
            unit = jnp.where(lane == below + (PANEL + 8 * t), 1.0, 0.0)
            aug.append(jnp.where(lane < PANEL, head[8 * t : 8 * t + 8, :128], unit))
        scale = [jnp.zeros((8, 128), jnp.float32) for _ in range(tiles)]
        for j in range(0, PANEL, BLOCK):
            block = range(BLOCK)
            first = j // 8
            cols = [
                {t: spread(aug[t][:, j + k : j + k + 1]) for t in range(first, tiles)}
                for k in block
            ]
            rows = []
            small = []
            for a in block:
                t, s = divmod(j + a, 8)
                rows.append(spread(aug[t][s : s + 1, :]))
                small.append([spread(cols[c][t][s : s + 1, :]) for c in range(a + 1)])
            recip = []
            for k in block:
                t, s = divmod(j + k, 8)
                recip.append(1.0 / small[k][k])
                scale[t] = jnp.where(below == s, lax.rsqrt(small[k][k]), scale[t])
                for a in range(k + 1, BLOCK):
                    ratio = small[a][k] * recip[k]
                    rows[a] = rows[a] - ratio * rows[k]
                    for c in range(k + 1, a + 1):
                        small[a][c] = small[a][c] - ratio * small[c][k]
            for t in range(first, tiles):
                for k in block:
                    if 8 * t + 7 <= j + k:
                        continue
                    factor = cols[k][t] * recip[k]
                    for c in range(k + 1, BLOCK):
                        cols[c][t] = cols[c][t] - factor * small[c][k]
                    if 8 * t <= j + k:
                        factor = jnp.where(below > j + k - 8 * t, factor, 0.0)
                    aug[t] = aug[t] - factor * rows[k]
        inverse = jnp.concatenate([x * y for x, y in zip(aug, scale)], axis=0)
        inverse = inverse[:, PANEL : 2 * PANEL]
        solved = jnp.dot(
            inverse, head, precision=lax.Precision.HIGHEST, preferred_element_type=jnp.float32
        )
        rolled = pltpu.roll(solved, lax.rem(step * PANEL + size, wide), axis=1)
        out_ref[pl.ds(pl.multiple_of(step * PANEL, PANEL), PANEL), :] = rolled[:, :size]
        left = jnp.where(wide_lane < size - step * PANEL, solved[:, :size], 0.0)
        change = lax.dot_general(
            left,
            solved,
            (((0,), (0,)), ((), ())),
            precision=lax.Precision.HIGHEST,
            preferred_element_type=jnp.float32,
        )
        fresh = work_ref[PANEL:, :] - change[PANEL:, :]
        work_ref[: size - PANEL, :] = pltpu.roll(fresh, wide - PANEL, axis=1)
        return carry

    lax.fori_loop(0, size // PANEL, panel, 0)


def inverse_factor(gram):
    size = gram.shape[0]
    return pl.pallas_call(
        inverse_factor_kernel,
        out_shape=jax.ShapeDtypeStruct((size, size), jnp.float32),
        in_specs=[pl.BlockSpec(memory_space=pltpu.VMEM)],
        out_specs=pl.BlockSpec(memory_space=pltpu.VMEM),
        scratch_shapes=[pltpu.VMEM((size, 2 * size), jnp.float32)],
        cost_estimate=pl.CostEstimate(
            flops=20000000000, bytes_accessed=8 * size * size, transcendentals=0
        ),
        name="inverse_factor",
    )(gram)


def sum_kernel(grads_ref, out_ref, held_ref, local_sem, send_sem, recv_sem):
    groups = held_ref.shape[0]
    quarter = held_ref.shape[3]
    me = lax.axis_index("dp")
    barrier = pltpu.get_barrier_semaphore()
    for d in range(1, groups):
        pl.semaphore_signal(
            barrier,
            inc=1,
            device_id={"dp": lax.rem(me + d, groups)},
            device_id_type=pl.DeviceIdType.MESH,
        )
    pl.semaphore_wait(barrier, groups - 1)

    def columns(who):
        return grads_ref.at[0, :, :, pl.ds(pl.multiple_of(who * quarter, quarter), quarter)]

    copies = []
    for d in range(1, groups):
        peer = lax.rem(me + d, groups)
        copy = pltpu.make_async_remote_copy(
            src_ref=columns(peer),
            dst_ref=held_ref.at[d],
            send_sem=send_sem.at[d - 1],
            recv_sem=recv_sem.at[d - 1],
            device_id={"dp": peer},
            device_id_type=pl.DeviceIdType.MESH,
        )
        copy.start()
        copies.append(copy)
    own = pltpu.make_async_copy(columns(me), held_ref.at[0], local_sem)
    own.start()
    own.wait()
    for copy in copies:
        copy.wait()
    step = 4

    def add(i, carry):
        at = pl.ds(i * step, step)
        total = held_ref[0, at].astype(jnp.float32)
        for d in range(1, groups):
            total = total + held_ref[d, at].astype(jnp.float32)
        for r in range(held_ref.shape[2] // 8):
            for c in range(quarter // 128):
                piece = total[:, 8 * r : 8 * r + 8, 128 * c : 128 * c + 128]
                out_ref[at, r * (quarter // 128) + c] = piece.astype(jnp.bfloat16)
        return carry

    lax.fori_loop(0, held_ref.shape[1] // step, add, 0)


def sum_quarters(grads, groups):
    _, count, shard, width = grads.shape
    quarter = width // groups
    pieces = shard * quarter // 1024
    return pl.pallas_call(
        sum_kernel,
        out_shape=jax.ShapeDtypeStruct((count, pieces, 8, 128), jnp.bfloat16),
        in_specs=[pl.BlockSpec(memory_space=pl.ANY)],
        out_specs=pl.BlockSpec(memory_space=pltpu.VMEM),
        scratch_shapes=[
            pltpu.VMEM((groups, count, shard, quarter), jnp.bfloat16),
            pltpu.SemaphoreType.DMA,
            pltpu.SemaphoreType.DMA((groups - 1,)),
            pltpu.SemaphoreType.DMA((groups - 1,)),
        ],
        compiler_params=pltpu.CompilerParams(collective_id=0, has_side_effects=True),
        cost_estimate=pl.CostEstimate(
            flops=20000000000, bytes_accessed=50000000, transcendentals=0
        ),
        name="sum_quarters",
    )(grads)


def pick_kernel(index_ref, data_ref, out_ref):
    count = out_ref.shape[0]

    def one(i, carry):
        place = index_ref[i]
        block = data_ref[jnp.maximum(place, 0)]
        out_ref[i] = jnp.where(place >= 0, block, jnp.zeros_like(block))
        return carry

    lax.fori_loop(0, count, one, 0, unroll=4)


def pick(index, data):
    return pl.pallas_call(
        pick_kernel,
        out_shape=jax.ShapeDtypeStruct((index.shape[0],) + data.shape[1:], data.dtype),
        in_specs=[
            pl.BlockSpec(memory_space=pltpu.SMEM),
            pl.BlockSpec(memory_space=pltpu.VMEM),
        ],
        out_specs=pl.BlockSpec(memory_space=pltpu.VMEM),
        name="pick",
    )(index, data)


def to_chunks(data):
    rows, cols = data.shape[-2:]
    lead = data.shape[:-2]
    n = len(lead)
    tiles = data.reshape(lead + (rows // 8, 8, cols // 128, 128))
    tiles = jnp.transpose(tiles, tuple(range(n)) + (n, n + 2, n + 1, n + 3))
    return tiles.reshape(lead + (rows // 8 * (cols // 128), 8, 128))


def from_chunks(data, rows, cols):
    lead = data.shape[:-3]
    n = len(lead)
    tiles = data.reshape(lead + (rows // 8, cols // 128, 8, 128))
    tiles = jnp.transpose(tiles, tuple(range(n)) + (n, n + 2, n + 1, n + 3))
    return tiles.reshape(lead + (rows, cols))


def exchange(data, axis=0):
    return lax.all_to_all(data, "rows", split_axis=axis, concat_axis=axis, tiled=True)


def per_device(grads, weight, basis, first_moment, second_moment, sketch, owner, rank):
    owners = lax.axis_size("rows")
    groups = lax.axis_size("dp")
    here = lax.axis_index("rows")
    capacity, rank_full, quarter = first_moment.shape
    count, shard, width = weight.shape
    total_rows = shard * owners
    root = float(total_rows) ** 0.5
    inverse_root = float(total_rows) ** (-0.5)
    slots = slot_of(owner, capacity)
    slot_ids = jnp.arange(capacity * owners, dtype=jnp.int32)
    hit = slots[:, None] == slot_ids[None, :]
    matrix_ids = jnp.arange(count, dtype=jnp.int32)
    source = jnp.max(jnp.where(hit, matrix_ids[:, None], -1), axis=0)
    pieces = shard * quarter // 1024

    moments = jnp.stack(
        [
            to_chunks(first_moment.astype(jnp.bfloat16)),
            to_chunks(second_moment.astype(jnp.bfloat16)),
        ],
        axis=2,
    )
    moments = jnp.transpose(moments, (1, 0, 2, 3, 4)).reshape(owners, 2 * capacity, 8, 128)
    sent = jnp.concatenate([moments, to_chunks(basis.astype(jnp.bfloat16))], axis=1)
    sent, grads = lax.optimization_barrier((sent, grads))
    first_trip = exchange(sent)
    moments = first_trip[:, : 2 * capacity].reshape(owners * capacity, 16, 128)
    old_basis = from_chunks(first_trip[:, 2 * capacity :], shard, rank_full)
    old_basis = old_basis.reshape(total_rows, rank_full)
    moments = pick(slots, moments).reshape(count, 2, 8, 128)

    mine = sum_quarters(grads, groups)

    second_trip = exchange(jnp.concatenate([mine, moments], axis=1))
    own = from_chunks(second_trip[:, :pieces], shard, quarter).reshape(total_rows, quarter)
    first_old = from_chunks(second_trip[:, pieces], rank_full, quarter).astype(jnp.float32)
    second_old = from_chunks(second_trip[:, pieces + 1], rank_full, quarter).astype(jnp.float32)
    whole = lax.all_gather(own, "dp", axis=1, tiled=True)

    projected = (
        lax.dot_general(
            old_basis, own, (((0,), (0,)), ((), ())), preferred_element_type=jnp.float32
        )
        * inverse_root
    )
    first_new = beta_one * first_old + (1.0 - beta_one) * projected
    second_new = beta_two * second_old + (1.0 - beta_two) * projected * projected
    my_rank = lax.dynamic_index_in_dim(rank, here, keepdims=False)
    keeping = (jnp.arange(rank_full, dtype=jnp.int32) < my_rank).astype(jnp.float32)[:, None]
    update = keeping * (first_new / bias_one) / (jnp.sqrt(second_new / bias_two) + epsilon)
    delta = (
        jnp.dot(old_basis, update.astype(jnp.bfloat16), preferred_element_type=jnp.float32)
        * inverse_root
    ).astype(jnp.bfloat16)

    third_trip = exchange(
        jnp.concatenate(
            [
                to_chunks(delta.reshape(owners, shard, quarter)),
                to_chunks(projected.astype(jnp.bfloat16))[:, None],
            ],
            axis=1,
        )
    )
    back_delta = from_chunks(third_trip[:, :pieces], shard, quarter)
    full_delta = lax.all_gather(back_delta, "dp", axis=2, tiled=True)
    spread = pick(source, third_trip[:, pieces]).reshape(owners, capacity, 8, 128)
    spread = jnp.transpose(exchange(spread), (1, 0, 2, 3))
    here_projected = from_chunks(spread, rank_full, quarter).astype(jnp.float32)
    matched = slots[:, None] == (here * capacity + jnp.arange(capacity, dtype=jnp.int32))[None, :]
    valid = jnp.any(matched, axis=0)[:, None, None]
    first_out = jnp.where(
        valid, beta_one * first_moment + (1.0 - beta_one) * here_projected, 0.0
    )
    second_out = jnp.where(
        valid,
        beta_two * second_moment + (1.0 - beta_two) * here_projected * here_projected,
        0.0,
    )

    sample = jnp.dot(whole, sketch, preferred_element_type=jnp.float32)
    gram = lax.dot_general(
        sample, sample, (((0,), (0,)), ((), ())), precision=lax.Precision.HIGHEST
    )
    inverse = inverse_factor(gram)
    solved = lax.dot_general(
        sample, inverse, (((1,), (1,)), ((), ())), precision=lax.Precision.HIGHEST
    )
    fresh = (solved * root).astype(jnp.bfloat16).reshape(owners, shard, rank_full)
    new_basis = exchange(fresh).astype(jnp.float32)
    new_weight = (weight.astype(jnp.float32) - step_size * full_delta.astype(jnp.float32)).astype(
        jnp.bfloat16
    )
    return (new_weight, new_basis, first_out, second_out)


def solution(mesh):
    in_specs = (
        P("dp", None, "rows", None),
        P(None, "rows", None),
        P(None, "rows", None),
        P("rows", None, "dp"),
        P("rows", None, "dp"),
        P(),
        P(),
        P(),
    )
    out_specs = (
        P(None, "rows", None),
        P(None, "rows", None),
        P("rows", None, "dp"),
        P("rows", None, "dp"),
    )
    return jax.shard_map(
        per_device, mesh=mesh, in_specs=in_specs, out_specs=out_specs, check_vma=False
    )
```

```python
import functools

import jax
import jax.numpy as jnp
from jax import lax
from jax.experimental import pallas as pl
from jax.experimental.pallas import tpu as pltpu
from jax.sharding import PartitionSpec as P

beta_one = 0.9
beta_two = 0.95
bias_one = 1.0 - 0.9**10
bias_two = 1.0 - 0.95**10
step_size = 0.5
epsilon = 1e-08

PANEL = 64
BLOCK = 8


def slot_of(owner, capacity):
    same = owner[:, None] == owner[None, :]
    places = jnp.arange(owner.shape[0], dtype=jnp.int32)
    earlier = places[None, :] < places[:, None]
    within = jnp.sum((same & earlier).astype(jnp.int32), axis=1)
    return owner * capacity + within


def inverse_factor_kernel(gram_ref, out_ref, work_ref):
    size = gram_ref.shape[0]
    wide = 2 * size
    work_ref[:, :size] = gram_ref[...]
    row = lax.broadcasted_iota(jnp.int32, (size, size), 0)
    col = lax.broadcasted_iota(jnp.int32, (size, size), 1)
    work_ref[:, size:] = jnp.where(row == col, 1.0, 0.0)
    lane = lax.broadcasted_iota(jnp.int32, (8, 128), 1)
    below = lax.broadcasted_iota(jnp.int32, (8, 128), 0)
    wide_lane = lax.broadcasted_iota(jnp.int32, (PANEL, size), 1)
    tiles = PANEL // 8

    def spread(line):
        return jnp.broadcast_to(line, (8, 128))

    def panel(step, carry):
        head = work_ref[:PANEL, :]
        aug = []
        for t in range(tiles):
            unit = jnp.where(lane == below + (PANEL + 8 * t), 1.0, 0.0)
            aug.append(jnp.where(lane < PANEL, head[8 * t : 8 * t + 8, :128], unit))
        scale = [jnp.zeros((8, 128), jnp.float32) for _ in range(tiles)]
        for j in range(0, PANEL, BLOCK):
            block = range(BLOCK)
            first = j // 8
            cols = [
                {t: spread(aug[t][:, j + k : j + k + 1]) for t in range(first, tiles)}
                for k in block
            ]
            rows = []
            small = []
            for a in block:
                t, s = divmod(j + a, 8)
                rows.append(spread(aug[t][s : s + 1, :]))
                small.append([spread(cols[c][t][s : s + 1, :]) for c in range(a + 1)])
            recip = []
            for k in block:
                t, s = divmod(j + k, 8)
                recip.append(1.0 / small[k][k])
                scale[t] = jnp.where(below == s, lax.rsqrt(small[k][k]), scale[t])
                for a in range(k + 1, BLOCK):
                    ratio = small[a][k] * recip[k]
                    rows[a] = rows[a] - ratio * rows[k]
                    for c in range(k + 1, a + 1):
                        small[a][c] = small[a][c] - ratio * small[c][k]
            for t in range(first, tiles):
                for k in block:
                    if 8 * t + 7 <= j + k:
                        continue
                    factor = cols[k][t] * recip[k]
                    for c in range(k + 1, BLOCK):
                        cols[c][t] = cols[c][t] - factor * small[c][k]
                    if 8 * t <= j + k:
                        factor = jnp.where(below > j + k - 8 * t, factor, 0.0)
                    aug[t] = aug[t] - factor * rows[k]
        inverse = jnp.concatenate([x * y for x, y in zip(aug, scale)], axis=0)
        inverse = inverse[:, PANEL : 2 * PANEL]
        solved = jnp.dot(
            inverse, head, precision=lax.Precision.HIGHEST, preferred_element_type=jnp.float32
        )
        rolled = pltpu.roll(solved, lax.rem(step * PANEL + size, wide), axis=1)
        out_ref[pl.ds(pl.multiple_of(step * PANEL, PANEL), PANEL), :] = rolled[:, :size]
        left = jnp.where(wide_lane < size - step * PANEL, solved[:, :size], 0.0)
        change = lax.dot_general(
            left,
            solved,
            (((0,), (0,)), ((), ())),
            precision=lax.Precision.HIGHEST,
            preferred_element_type=jnp.float32,
        )
        fresh = work_ref[PANEL:, :] - change[PANEL:, :]
        work_ref[: size - PANEL, :] = pltpu.roll(fresh, wide - PANEL, axis=1)
        return carry

    lax.fori_loop(0, size // PANEL, panel, 0)


def greet(groups):
    me = lax.axis_index("dp")
    barrier = pltpu.get_barrier_semaphore()
    for d in range(1, groups):
        pl.semaphore_signal(
            barrier,
            inc=1,
            device_id={"dp": lax.rem(me + d, groups)},
            device_id_type=pl.DeviceIdType.MESH,
        )
    pl.semaphore_wait(barrier, groups - 1)
    return me


def push(source, target, send_sem, recv_sem, peer):
    copy = pltpu.make_async_remote_copy(
        src_ref=source,
        dst_ref=target,
        send_sem=send_sem,
        recv_sem=recv_sem,
        device_id={"dp": peer},
        device_id_type=pl.DeviceIdType.MESH,
    )
    copy.start()
    return copy


def refresh_kernel(
    root, part_ref, out_ref, held_ref, whole_ref, grams_ref, gram_ref, inverse_ref, work_ref, sems
):
    total, rank_full = part_ref.shape
    block = held_ref.shape[1]
    groups = total // block
    me = greet(groups)

    def rows(ref, who):
        return ref.at[pl.ds(pl.multiple_of(who * block, block), block)]

    copies = []
    for d in range(1, groups):
        peer = lax.rem(me + d, groups)
        copies.append(
            push(rows(part_ref, peer), held_ref.at[d - 1], sems.at[0, d], sems.at[1, d], peer)
        )
    for copy in copies:
        copy.wait()
    mine = rows(part_ref, me)[...].astype(jnp.float32)
    for d in range(1, groups):
        mine = mine + held_ref[d - 1].astype(jnp.float32)
    mine = mine.astype(jnp.bfloat16)
    rows(whole_ref, me)[...] = mine
    contract = (((0,), (0,)), ((), ()))
    grams_ref[me] = lax.dot_general(mine, mine, contract, preferred_element_type=jnp.float32)
    copies = []
    for d in range(1, groups):
        peer = lax.rem(me + d, groups)
        copies.append(
            push(rows(whole_ref, me), rows(whole_ref, me), sems.at[2, d], sems.at[3, d], peer)
        )
    for copy in copies:
        copy.wait()
    for d in range(1, groups):
        who = lax.rem(me + d, groups)
        other = rows(whole_ref, who)[...]
        grams_ref[who] = lax.dot_general(
            other, other, contract, preferred_element_type=jnp.float32
        )
    gram = grams_ref[0]
    for b in range(1, groups):
        gram = gram + grams_ref[b]
    gram_ref[...] = gram
    inverse_factor_kernel(gram_ref, inverse_ref, work_ref)
    inverse = inverse_ref[...] * root
    high = inverse.astype(jnp.bfloat16)
    low = (inverse - high.astype(jnp.float32)).astype(jnp.bfloat16)
    contract = (((1,), (1,)), ((), ()))
    for b in range(groups):
        data = whole_ref[b * block : (b + 1) * block]
        fresh = lax.dot_general(data, high, contract, preferred_element_type=jnp.float32)
        fresh += lax.dot_general(data, low, contract, preferred_element_type=jnp.float32)
        fresh = fresh.reshape(block // 8, 8, rank_full)
        for c in range(rank_full // 128):
            piece = fresh[:, :, 128 * c : 128 * c + 128].astype(jnp.bfloat16)
            out_ref[b * (block // 8) : (b + 1) * (block // 8), c] = piece


def refresh(part, groups, root):
    total, rank_full = part.shape
    block = total // groups
    return pl.pallas_call(
        functools.partial(refresh_kernel, root),
        out_shape=jax.ShapeDtypeStruct((total // 8, rank_full // 128, 8, 128), jnp.bfloat16),
        in_specs=[pl.BlockSpec(memory_space=pltpu.VMEM)],
        out_specs=pl.BlockSpec(memory_space=pltpu.VMEM),
        scratch_shapes=[
            pltpu.VMEM((groups - 1, block, rank_full), jnp.bfloat16),
            pltpu.VMEM((total, rank_full), jnp.bfloat16),
            pltpu.VMEM((groups, rank_full, rank_full), jnp.float32),
            pltpu.VMEM((rank_full, rank_full), jnp.float32),
            pltpu.VMEM((rank_full, rank_full), jnp.float32),
            pltpu.VMEM((rank_full, 2 * rank_full), jnp.float32),
            pltpu.SemaphoreType.DMA((4, groups)),
        ],
        compiler_params=pltpu.CompilerParams(collective_id=1, has_side_effects=True),
        cost_estimate=pl.CostEstimate(
            flops=20000000000, bytes_accessed=50000000, transcendentals=0
        ),
        name="refresh",
    )(part)


def gather_kernel(groups, mine_ref, out_ref, local_sem, send_sem, recv_sem):
    quarter = mine_ref.shape[2]
    me = greet(groups)
    columns = out_ref.at[:, :, pl.ds(pl.multiple_of(me * quarter, quarter), quarter)]
    copies = []
    for d in range(1, groups):
        peer = lax.rem(me + d, groups)
        copies.append(push(mine_ref, columns, send_sem.at[d - 1], recv_sem.at[d - 1], peer))
    own = pltpu.make_async_copy(mine_ref, columns, local_sem)
    own.start()
    own.wait()
    for copy in copies:
        copy.wait()


def gather_quarters(mine, groups):
    count, shard, quarter = mine.shape
    return pl.pallas_call(
        functools.partial(gather_kernel, groups),
        out_shape=jax.ShapeDtypeStruct((count, shard, quarter * groups), mine.dtype),
        in_specs=[pl.BlockSpec(memory_space=pltpu.VMEM)],
        out_specs=pl.BlockSpec(memory_space=pl.ANY),
        scratch_shapes=[
            pltpu.SemaphoreType.DMA,
            pltpu.SemaphoreType.DMA((groups - 1,)),
            pltpu.SemaphoreType.DMA((groups - 1,)),
        ],
        compiler_params=pltpu.CompilerParams(collective_id=2, has_side_effects=True),
        cost_estimate=pl.CostEstimate(
            flops=20000000000, bytes_accessed=50000000, transcendentals=0
        ),
        name="gather_quarters",
    )(mine)


def sum_kernel(grads_ref, out_ref, held_ref, local_sem, send_sem, recv_sem):
    groups = held_ref.shape[0]
    quarter = held_ref.shape[3]
    me = lax.axis_index("dp")
    barrier = pltpu.get_barrier_semaphore()
    for d in range(1, groups):
        pl.semaphore_signal(
            barrier,
            inc=1,
            device_id={"dp": lax.rem(me + d, groups)},
            device_id_type=pl.DeviceIdType.MESH,
        )
    pl.semaphore_wait(barrier, groups - 1)

    def columns(who):
        return grads_ref.at[0, :, :, pl.ds(pl.multiple_of(who * quarter, quarter), quarter)]

    copies = []
    for d in range(1, groups):
        peer = lax.rem(me + d, groups)
        copy = pltpu.make_async_remote_copy(
            src_ref=columns(peer),
            dst_ref=held_ref.at[d],
            send_sem=send_sem.at[d - 1],
            recv_sem=recv_sem.at[d - 1],
            device_id={"dp": peer},
            device_id_type=pl.DeviceIdType.MESH,
        )
        copy.start()
        copies.append(copy)
    own = pltpu.make_async_copy(columns(me), held_ref.at[0], local_sem)
    own.start()
    own.wait()
    for copy in copies:
        copy.wait()
    step = 4

    def add(i, carry):
        at = pl.ds(i * step, step)
        total = held_ref[0, at].astype(jnp.float32)
        for d in range(1, groups):
            total = total + held_ref[d, at].astype(jnp.float32)
        for r in range(held_ref.shape[2] // 8):
            for c in range(quarter // 128):
                piece = total[:, 8 * r : 8 * r + 8, 128 * c : 128 * c + 128]
                out_ref[at, r * (quarter // 128) + c] = piece.astype(jnp.bfloat16)
        return carry

    lax.fori_loop(0, held_ref.shape[1] // step, add, 0)


def sum_quarters(grads, groups):
    _, count, shard, width = grads.shape
    quarter = width // groups
    pieces = shard * quarter // 1024
    return pl.pallas_call(
        sum_kernel,
        out_shape=jax.ShapeDtypeStruct((count, pieces, 8, 128), jnp.bfloat16),
        in_specs=[pl.BlockSpec(memory_space=pl.ANY)],
        out_specs=pl.BlockSpec(memory_space=pltpu.VMEM),
        scratch_shapes=[
            pltpu.VMEM((groups, count, shard, quarter), jnp.bfloat16),
            pltpu.SemaphoreType.DMA,
            pltpu.SemaphoreType.DMA((groups - 1,)),
            pltpu.SemaphoreType.DMA((groups - 1,)),
        ],
        compiler_params=pltpu.CompilerParams(collective_id=0, has_side_effects=True),
        cost_estimate=pl.CostEstimate(
            flops=20000000000, bytes_accessed=50000000, transcendentals=0
        ),
        name="sum_quarters",
    )(grads)


def pick_kernel(index_ref, data_ref, out_ref):
    count = out_ref.shape[0]

    def one(i, carry):
        place = index_ref[i]
        block = data_ref[jnp.maximum(place, 0)]
        out_ref[i] = jnp.where(place >= 0, block, jnp.zeros_like(block))
        return carry

    lax.fori_loop(0, count, one, 0, unroll=4)


def pick(index, data):
    return pl.pallas_call(
        pick_kernel,
        out_shape=jax.ShapeDtypeStruct((index.shape[0],) + data.shape[1:], data.dtype),
        in_specs=[
            pl.BlockSpec(memory_space=pltpu.SMEM),
            pl.BlockSpec(memory_space=pltpu.VMEM),
        ],
        out_specs=pl.BlockSpec(memory_space=pltpu.VMEM),
        name="pick",
    )(index, data)


def to_chunks(data):
    rows, cols = data.shape[-2:]
    lead = data.shape[:-2]
    n = len(lead)
    tiles = data.reshape(lead + (rows // 8, 8, cols // 128, 128))
    tiles = jnp.transpose(tiles, tuple(range(n)) + (n, n + 2, n + 1, n + 3))
    return tiles.reshape(lead + (rows // 8 * (cols // 128), 8, 128))


def from_chunks(data, rows, cols):
    lead = data.shape[:-3]
    n = len(lead)
    tiles = data.reshape(lead + (rows // 8, cols // 128, 8, 128))
    tiles = jnp.transpose(tiles, tuple(range(n)) + (n, n + 2, n + 1, n + 3))
    return tiles.reshape(lead + (rows, cols))


def exchange(data, axis=0):
    return lax.all_to_all(data, "rows", split_axis=axis, concat_axis=axis, tiled=True)


def per_device(grads, weight, basis, first_moment, second_moment, sketch, owner, rank):
    owners = lax.axis_size("rows")
    groups = lax.axis_size("dp")
    here = lax.axis_index("rows")
    capacity, rank_full, quarter = first_moment.shape
    count, shard, width = weight.shape
    total_rows = shard * owners
    root = float(total_rows) ** 0.5
    inverse_root = float(total_rows) ** (-0.5)
    slots = slot_of(owner, capacity)
    slot_ids = jnp.arange(capacity * owners, dtype=jnp.int32)
    hit = slots[:, None] == slot_ids[None, :]
    matrix_ids = jnp.arange(count, dtype=jnp.int32)
    source = jnp.max(jnp.where(hit, matrix_ids[:, None], -1), axis=0)
    pieces = shard * quarter // 1024

    moments = jnp.stack(
        [
            to_chunks(first_moment.astype(jnp.bfloat16)),
            to_chunks(second_moment.astype(jnp.bfloat16)),
        ],
        axis=2,
    )
    moments = jnp.transpose(moments, (1, 0, 2, 3, 4)).reshape(owners, 2 * capacity, 8, 128)
    sent = jnp.concatenate([moments, to_chunks(basis.astype(jnp.bfloat16))], axis=1)
    sent, grads = lax.optimization_barrier((sent, grads))
    first_trip = exchange(sent)
    moments = first_trip[:, : 2 * capacity].reshape(owners * capacity, 16, 128)
    old_basis = from_chunks(first_trip[:, 2 * capacity :], shard, rank_full)
    old_basis = old_basis.reshape(total_rows, rank_full)
    moments = pick(slots, moments).reshape(count, 2, 8, 128)

    mine = sum_quarters(grads, groups)

    second_trip = exchange(jnp.concatenate([mine, moments], axis=1))
    own = from_chunks(second_trip[:, :pieces], shard, quarter).reshape(total_rows, quarter)
    first_old = from_chunks(second_trip[:, pieces], rank_full, quarter).astype(jnp.float32)
    second_old = from_chunks(second_trip[:, pieces + 1], rank_full, quarter).astype(jnp.float32)
    sketch_part = lax.dynamic_slice_in_dim(sketch, lax.axis_index("dp") * quarter, quarter, 0)
    part = jnp.dot(own, sketch_part, preferred_element_type=jnp.float32).astype(jnp.bfloat16)

    projected = (
        lax.dot_general(
            old_basis, own, (((0,), (0,)), ((), ())), preferred_element_type=jnp.float32
        )
        * inverse_root
    )
    first_new = beta_one * first_old + (1.0 - beta_one) * projected
    second_new = beta_two * second_old + (1.0 - beta_two) * projected * projected
    my_rank = lax.dynamic_index_in_dim(rank, here, keepdims=False)
    keeping = (jnp.arange(rank_full, dtype=jnp.int32) < my_rank).astype(jnp.float32)[:, None]
    update = keeping * (first_new / bias_one) / (jnp.sqrt(second_new / bias_two) + epsilon)
    delta = (
        jnp.dot(old_basis, update.astype(jnp.bfloat16), preferred_element_type=jnp.float32)
        * inverse_root
    ).astype(jnp.bfloat16)

    sent = jnp.concatenate(
        [
            to_chunks(delta.reshape(owners, shard, quarter)),
            to_chunks(projected.astype(jnp.bfloat16))[:, None],
        ],
        axis=1,
    )
    sent, part = lax.optimization_barrier((sent, part))
    third_trip = exchange(sent)
    fresh = refresh(part, groups, root).reshape(owners, shard * rank_full // 1024, 8, 128)

    spread = pick(source, third_trip[:, pieces]).reshape(owners, capacity, 8, 128)
    sent = jnp.concatenate([spread, fresh], axis=1)
    back_delta = from_chunks(third_trip[:, :pieces], shard, quarter)
    sent, back_delta = lax.optimization_barrier((sent, back_delta))
    fourth_trip = exchange(sent)
    full_delta = gather_quarters(back_delta, groups)
    new_weight = (weight.astype(jnp.float32) - step_size * full_delta.astype(jnp.float32)).astype(
        jnp.bfloat16
    )
    new_basis = from_chunks(fourth_trip[:, capacity:], shard, rank_full).astype(jnp.float32)
    spread = jnp.transpose(fourth_trip[:, :capacity], (1, 0, 2, 3))
    here_projected = from_chunks(spread, rank_full, quarter).astype(jnp.float32)
    matched = slots[:, None] == (here * capacity + jnp.arange(capacity, dtype=jnp.int32))[None, :]
    valid = jnp.any(matched, axis=0)[:, None, None]
    first_out = jnp.where(
        valid, beta_one * first_moment + (1.0 - beta_one) * here_projected, 0.0
    )
    second_out = jnp.where(
        valid,
        beta_two * second_moment + (1.0 - beta_two) * here_projected * here_projected,
        0.0,
    )

    return (new_weight, new_basis, first_out, second_out)


def solution(mesh):
    in_specs = (
        P("dp", None, "rows", None),
        P(None, "rows", None),
        P(None, "rows", None),
        P("rows", None, "dp"),
        P("rows", None, "dp"),
        P(),
        P(),
        P(),
    )
    out_specs = (
        P(None, "rows", None),
        P(None, "rows", None),
        P("rows", None, "dp"),
        P("rows", None, "dp"),
    )
    return jax.shard_map(
        per_device, mesh=mesh, in_specs=in_specs, out_specs=out_specs, check_vma=False
    )
```

```python
import functools

import jax
import jax.numpy as jnp
from jax import lax
from jax.experimental import pallas as pl
from jax.experimental.pallas import tpu as pltpu
from jax.sharding import PartitionSpec as P

beta_one = 0.9
beta_two = 0.95
bias_one = 1.0 - 0.9**10
bias_two = 1.0 - 0.95**10
step_size = 0.5
epsilon = 1e-08

PANEL = 64
BLOCK = 8


def slot_of(owner, capacity):
    same = owner[:, None] == owner[None, :]
    places = jnp.arange(owner.shape[0], dtype=jnp.int32)
    earlier = places[None, :] < places[:, None]
    within = jnp.sum((same & earlier).astype(jnp.int32), axis=1)
    return owner * capacity + within


def inverse_factor_kernel(gram_ref, out_ref, work_ref):
    size = gram_ref.shape[0]
    wide = 2 * size
    work_ref[:, :size] = gram_ref[...]
    row = lax.broadcasted_iota(jnp.int32, (size, size), 0)
    col = lax.broadcasted_iota(jnp.int32, (size, size), 1)
    work_ref[:, size:] = jnp.where(row == col, 1.0, 0.0)
    lane = lax.broadcasted_iota(jnp.int32, (8, 128), 1)
    below = lax.broadcasted_iota(jnp.int32, (8, 128), 0)
    wide_lane = lax.broadcasted_iota(jnp.int32, (PANEL, size), 1)
    tiles = PANEL // 8

    def spread(line):
        return jnp.broadcast_to(line, (8, 128))

    def panel(step, carry):
        head = work_ref[:PANEL, :]
        aug = []
        for t in range(tiles):
            unit = jnp.where(lane == below + (PANEL + 8 * t), 1.0, 0.0)
            aug.append(jnp.where(lane < PANEL, head[8 * t : 8 * t + 8, :128], unit))
        scale = [jnp.zeros((8, 128), jnp.float32) for _ in range(tiles)]
        for j in range(0, PANEL, BLOCK):
            block = range(BLOCK)
            first = j // 8
            cols = [
                {t: spread(aug[t][:, j + k : j + k + 1]) for t in range(first, tiles)}
                for k in block
            ]
            rows = []
            small = []
            for a in block:
                t, s = divmod(j + a, 8)
                rows.append(spread(aug[t][s : s + 1, :]))
                small.append([spread(cols[c][t][s : s + 1, :]) for c in range(a + 1)])
            recip = []
            for k in block:
                t, s = divmod(j + k, 8)
                recip.append(1.0 / small[k][k])
                scale[t] = jnp.where(below == s, lax.rsqrt(small[k][k]), scale[t])
                for a in range(k + 1, BLOCK):
                    ratio = small[a][k] * recip[k]
                    rows[a] = rows[a] - ratio * rows[k]
                    for c in range(k + 1, a + 1):
                        small[a][c] = small[a][c] - ratio * small[c][k]
            for t in range(first, tiles):
                for k in block:
                    if 8 * t + 7 <= j + k:
                        continue
                    factor = cols[k][t] * recip[k]
                    for c in range(k + 1, BLOCK):
                        cols[c][t] = cols[c][t] - factor * small[c][k]
                    if 8 * t <= j + k:
                        factor = jnp.where(below > j + k - 8 * t, factor, 0.0)
                    aug[t] = aug[t] - factor * rows[k]
        inverse = jnp.concatenate([x * y for x, y in zip(aug, scale)], axis=0)
        inverse = inverse[:, PANEL : 2 * PANEL]
        solved = jnp.dot(
            inverse, head, precision=lax.Precision.HIGHEST, preferred_element_type=jnp.float32
        )
        rolled = pltpu.roll(solved, lax.rem(step * PANEL + size, wide), axis=1)
        out_ref[pl.ds(pl.multiple_of(step * PANEL, PANEL), PANEL), :] = rolled[:, :size]
        left = jnp.where(wide_lane < size - step * PANEL, solved[:, :size], 0.0)
        change = lax.dot_general(
            left,
            solved,
            (((0,), (0,)), ((), ())),
            precision=lax.Precision.HIGHEST,
            preferred_element_type=jnp.float32,
        )
        fresh = work_ref[PANEL:, :] - change[PANEL:, :]
        work_ref[: size - PANEL, :] = pltpu.roll(fresh, wide - PANEL, axis=1)
        return carry

    lax.fori_loop(0, size // PANEL, panel, 0)


def greet(groups):
    me = lax.axis_index("dp")
    barrier = pltpu.get_barrier_semaphore()
    for d in range(1, groups):
        pl.semaphore_signal(
            barrier,
            inc=1,
            device_id={"dp": lax.rem(me + d, groups)},
            device_id_type=pl.DeviceIdType.MESH,
        )
    pl.semaphore_wait(barrier, groups - 1)
    return me


def push(source, target, send_sem, recv_sem, peer):
    copy = pltpu.make_async_remote_copy(
        src_ref=source,
        dst_ref=target,
        send_sem=send_sem,
        recv_sem=recv_sem,
        device_id={"dp": peer},
        device_id_type=pl.DeviceIdType.MESH,
    )
    copy.start()
    return copy


def refresh_kernel(
    root, part_ref, out_ref, held_ref, whole_ref, grams_ref, gram_ref, inverse_ref, work_ref, sems
):
    total, rank_full = part_ref.shape
    block = held_ref.shape[1]
    groups = total // block
    me = greet(groups)

    def rows(ref, who):
        return ref.at[pl.ds(pl.multiple_of(who * block, block), block)]

    copies = []
    for d in range(1, groups):
        peer = lax.rem(me + d, groups)
        copies.append(
            push(rows(part_ref, peer), held_ref.at[d - 1], sems.at[0, d], sems.at[1, d], peer)
        )
    for copy in copies:
        copy.wait()
    mine = rows(part_ref, me)[...].astype(jnp.float32)
    for d in range(1, groups):
        mine = mine + held_ref[d - 1].astype(jnp.float32)
    mine = mine.astype(jnp.bfloat16)
    rows(whole_ref, me)[...] = mine
    contract = (((0,), (0,)), ((), ()))
    grams_ref[me] = lax.dot_general(mine, mine, contract, preferred_element_type=jnp.float32)
    copies = []
    for d in range(1, groups):
        peer = lax.rem(me + d, groups)
        copies.append(
            push(rows(whole_ref, me), rows(whole_ref, me), sems.at[2, d], sems.at[3, d], peer)
        )
    for copy in copies:
        copy.wait()
    for d in range(1, groups):
        who = lax.rem(me + d, groups)
        other = rows(whole_ref, who)[...]
        grams_ref[who] = lax.dot_general(
            other, other, contract, preferred_element_type=jnp.float32
        )
    gram = grams_ref[0]
    for b in range(1, groups):
        gram = gram + grams_ref[b]
    gram_ref[...] = gram
    inverse_factor_kernel(gram_ref, inverse_ref, work_ref)
    inverse = inverse_ref[...] * root
    high = inverse.astype(jnp.bfloat16)
    low = (inverse - high.astype(jnp.float32)).astype(jnp.bfloat16)
    contract = (((1,), (1,)), ((), ()))
    for b in range(groups):
        data = whole_ref[b * block : (b + 1) * block]
        fresh = lax.dot_general(data, high, contract, preferred_element_type=jnp.float32)
        fresh += lax.dot_general(data, low, contract, preferred_element_type=jnp.float32)
        fresh = fresh.reshape(block // 8, 8, rank_full)
        for c in range(rank_full // 128):
            piece = fresh[:, :, 128 * c : 128 * c + 128].astype(jnp.bfloat16)
            out_ref[b * (block // 8) : (b + 1) * (block // 8), c] = piece


def refresh(part, groups, root):
    total, rank_full = part.shape
    block = total // groups
    return pl.pallas_call(
        functools.partial(refresh_kernel, root),
        out_shape=jax.ShapeDtypeStruct((total // 8, rank_full // 128, 8, 128), jnp.bfloat16),
        in_specs=[pl.BlockSpec(memory_space=pltpu.VMEM)],
        out_specs=pl.BlockSpec(memory_space=pltpu.VMEM),
        scratch_shapes=[
            pltpu.VMEM((groups - 1, block, rank_full), jnp.bfloat16),
            pltpu.VMEM((total, rank_full), jnp.bfloat16),
            pltpu.VMEM((groups, rank_full, rank_full), jnp.float32),
            pltpu.VMEM((rank_full, rank_full), jnp.float32),
            pltpu.VMEM((rank_full, rank_full), jnp.float32),
            pltpu.VMEM((rank_full, 2 * rank_full), jnp.float32),
            pltpu.SemaphoreType.DMA((4, groups)),
        ],
        compiler_params=pltpu.CompilerParams(collective_id=1, has_side_effects=True),
        cost_estimate=pl.CostEstimate(
            flops=20000000000, bytes_accessed=50000000, transcendentals=0
        ),
        name="refresh",
    )(part)


def gather_kernel(groups, stacked, mine_ref, out_ref, local_sem, send_sem, recv_sem):
    count = mine_ref.shape[0]
    half = count // 2
    quarter = mine_ref.shape[2]
    me = lax.axis_index("dp")
    right = lax.rem(me + 1, groups)
    left = lax.rem(me + groups - 1, groups)
    barrier = pltpu.get_barrier_semaphore()
    for peer in (left, right):
        pl.semaphore_signal(
            barrier, inc=1, device_id={"dp": peer}, device_id_type=pl.DeviceIdType.MESH
        )
    pl.semaphore_wait(barrier, 2)

    def place(who, first, size):
        if stacked:
            return out_ref.at[who, pl.ds(first, size)]
        columns = pl.ds(pl.multiple_of(who * quarter, quarter), quarter)
        return out_ref.at[pl.ds(first, size), :, columns]

    def send(way, h):
        return push(
            mine_ref.at[pl.ds(h * half, half)],
            place(me, h * half, half),
            send_sem.at[way, h],
            recv_sem.at[way, h],
            (right, left)[way],
        )

    copies = [send(0, 0), send(1, 1), send(0, 1), send(1, 0)]
    own = pltpu.make_async_copy(mine_ref, place(me, 0, count), local_sem)
    own.start()
    copies[0].wait_recv()
    block = place(left, 0, half)
    onward = push(block, block, send_sem.at[0, 2], recv_sem.at[0, 2], right)
    copies[1].wait_recv()
    block = place(right, half, half)
    backward = push(block, block, send_sem.at[1, 2], recv_sem.at[1, 2], left)
    copies[2].wait_recv()
    copies[3].wait_recv()
    for copy in copies:
        copy.wait_send()
    onward.wait()
    backward.wait()
    own.wait()


def gather_quarters(mine, groups, stacked, number):
    assert groups == 4
    count, shard, quarter = mine.shape
    shape = (groups,) + mine.shape if stacked else (count, shard, quarter * groups)
    return pl.pallas_call(
        functools.partial(gather_kernel, groups, stacked),
        out_shape=jax.ShapeDtypeStruct(shape, mine.dtype),
        in_specs=[pl.BlockSpec(memory_space=pltpu.VMEM)],
        out_specs=pl.BlockSpec(memory_space=pl.ANY),
        scratch_shapes=[
            pltpu.SemaphoreType.DMA,
            pltpu.SemaphoreType.DMA((2, 3)),
            pltpu.SemaphoreType.DMA((2, 3)),
        ],
        compiler_params=pltpu.CompilerParams(collective_id=number, has_side_effects=True),
        cost_estimate=pl.CostEstimate(
            flops=20000000000, bytes_accessed=50000000, transcendentals=0
        ),
        name="gather_tiles" if stacked else "gather_quarters",
    )(mine)


def sum_kernel(grads_ref, out_ref, held_ref, local_sem, send_sem, recv_sem):
    groups = held_ref.shape[0]
    quarter = held_ref.shape[3]
    me = lax.axis_index("dp")
    barrier = pltpu.get_barrier_semaphore()
    for d in range(1, groups):
        pl.semaphore_signal(
            barrier,
            inc=1,
            device_id={"dp": lax.rem(me + d, groups)},
            device_id_type=pl.DeviceIdType.MESH,
        )
    pl.semaphore_wait(barrier, groups - 1)

    def columns(who):
        return grads_ref.at[0, :, :, pl.ds(pl.multiple_of(who * quarter, quarter), quarter)]

    copies = []
    for d in range(1, groups):
        peer = lax.rem(me + d, groups)
        copy = pltpu.make_async_remote_copy(
            src_ref=columns(peer),
            dst_ref=held_ref.at[d],
            send_sem=send_sem.at[d - 1],
            recv_sem=recv_sem.at[d - 1],
            device_id={"dp": peer},
            device_id_type=pl.DeviceIdType.MESH,
        )
        copy.start()
        copies.append(copy)
    own = pltpu.make_async_copy(columns(me), held_ref.at[0], local_sem)
    own.start()
    own.wait()
    for copy in copies:
        copy.wait()
    step = 4

    def add(i, carry):
        at = pl.ds(i * step, step)
        total = held_ref[0, at].astype(jnp.float32)
        for d in range(1, groups):
            total = total + held_ref[d, at].astype(jnp.float32)
        for r in range(held_ref.shape[2] // 8):
            for c in range(quarter // 128):
                piece = total[:, 8 * r : 8 * r + 8, 128 * c : 128 * c + 128]
                out_ref[at, r * (quarter // 128) + c] = piece.astype(jnp.bfloat16)
        return carry

    lax.fori_loop(0, held_ref.shape[1] // step, add, 0)


def sum_quarters(grads, groups):
    _, count, shard, width = grads.shape
    quarter = width // groups
    pieces = shard * quarter // 1024
    return pl.pallas_call(
        sum_kernel,
        out_shape=jax.ShapeDtypeStruct((count, pieces, 8, 128), jnp.bfloat16),
        in_specs=[pl.BlockSpec(memory_space=pl.ANY)],
        out_specs=pl.BlockSpec(memory_space=pltpu.VMEM),
        scratch_shapes=[
            pltpu.VMEM((groups, count, shard, quarter), jnp.bfloat16),
            pltpu.SemaphoreType.DMA,
            pltpu.SemaphoreType.DMA((groups - 1,)),
            pltpu.SemaphoreType.DMA((groups - 1,)),
        ],
        compiler_params=pltpu.CompilerParams(collective_id=0, has_side_effects=True),
        cost_estimate=pl.CostEstimate(
            flops=20000000000, bytes_accessed=50000000, transcendentals=0
        ),
        name="sum_quarters",
    )(grads)


def pick_kernel(index_ref, data_ref, out_ref):
    count = out_ref.shape[0]

    def one(i, carry):
        place = index_ref[i]
        block = data_ref[jnp.maximum(place, 0)]
        out_ref[i] = jnp.where(place >= 0, block, jnp.zeros_like(block))
        return carry

    lax.fori_loop(0, count, one, 0, unroll=4)


def pick(index, data):
    return pl.pallas_call(
        pick_kernel,
        out_shape=jax.ShapeDtypeStruct((index.shape[0],) + data.shape[1:], data.dtype),
        in_specs=[
            pl.BlockSpec(memory_space=pltpu.SMEM),
            pl.BlockSpec(memory_space=pltpu.VMEM),
        ],
        out_specs=pl.BlockSpec(memory_space=pltpu.VMEM),
        name="pick",
    )(index, data)


def to_chunks(data):
    rows, cols = data.shape[-2:]
    lead = data.shape[:-2]
    n = len(lead)
    tiles = data.reshape(lead + (rows // 8, 8, cols // 128, 128))
    tiles = jnp.transpose(tiles, tuple(range(n)) + (n, n + 2, n + 1, n + 3))
    return tiles.reshape(lead + (rows // 8 * (cols // 128), 8, 128))


def from_chunks(data, rows, cols):
    lead = data.shape[:-3]
    n = len(lead)
    tiles = data.reshape(lead + (rows // 8, cols // 128, 8, 128))
    tiles = jnp.transpose(tiles, tuple(range(n)) + (n, n + 2, n + 1, n + 3))
    return tiles.reshape(lead + (rows, cols))


def exchange(data, axis=0):
    return lax.all_to_all(data, "rows", split_axis=axis, concat_axis=axis, tiled=True)


def per_device(grads, weight, basis, first_moment, second_moment, sketch, owner, rank):
    owners = lax.axis_size("rows")
    groups = lax.axis_size("dp")
    here = lax.axis_index("rows")
    capacity, rank_full, quarter = first_moment.shape
    count, shard, width = weight.shape
    total_rows = shard * owners
    root = float(total_rows) ** 0.5
    inverse_root = float(total_rows) ** (-0.5)
    slots = slot_of(owner, capacity)
    slot_ids = jnp.arange(capacity * owners, dtype=jnp.int32)
    hit = slots[:, None] == slot_ids[None, :]
    matrix_ids = jnp.arange(count, dtype=jnp.int32)
    source = jnp.max(jnp.where(hit, matrix_ids[:, None], -1), axis=0)
    pieces = shard * quarter // 1024

    moments = jnp.stack(
        [
            to_chunks(first_moment.astype(jnp.bfloat16)),
            to_chunks(second_moment.astype(jnp.bfloat16)),
        ],
        axis=2,
    )
    moments = jnp.transpose(moments, (1, 0, 2, 3, 4)).reshape(owners, 2 * capacity, 8, 128)
    tile = lax.dynamic_slice_in_dim(
        to_chunks(basis.astype(jnp.bfloat16)), lax.axis_index("dp"), 1, 1
    )
    sent = jnp.concatenate([moments, tile], axis=1)
    sent, grads = lax.optimization_barrier((sent, grads))
    first_trip = exchange(sent)
    moments = first_trip[:, : 2 * capacity].reshape(owners * capacity, 16, 128)
    tile = first_trip[:, 2 * capacity]
    moments = pick(slots, moments).reshape(count, 2, 8, 128)

    mine = sum_quarters(grads, groups)

    sent = jnp.concatenate([mine, moments], axis=1)
    sent, tile = lax.optimization_barrier((sent, tile))
    second_trip = exchange(sent)
    old_basis = jnp.transpose(gather_quarters(tile, groups, True, 3), (1, 0, 2, 3))
    old_basis = from_chunks(old_basis, shard, rank_full).reshape(total_rows, rank_full)
    own = from_chunks(second_trip[:, :pieces], shard, quarter).reshape(total_rows, quarter)
    first_old = from_chunks(second_trip[:, pieces], rank_full, quarter).astype(jnp.float32)
    second_old = from_chunks(second_trip[:, pieces + 1], rank_full, quarter).astype(jnp.float32)
    sketch_part = lax.dynamic_slice_in_dim(sketch, lax.axis_index("dp") * quarter, quarter, 0)
    part = jnp.dot(own, sketch_part, preferred_element_type=jnp.float32).astype(jnp.bfloat16)

    projected = (
        lax.dot_general(
            old_basis, own, (((0,), (0,)), ((), ())), preferred_element_type=jnp.float32
        )
        * inverse_root
    )
    first_new = beta_one * first_old + (1.0 - beta_one) * projected
    second_new = beta_two * second_old + (1.0 - beta_two) * projected * projected
    my_rank = lax.dynamic_index_in_dim(rank, here, keepdims=False)
    keeping = (jnp.arange(rank_full, dtype=jnp.int32) < my_rank).astype(jnp.float32)[:, None]
    update = keeping * (first_new / bias_one) / (jnp.sqrt(second_new / bias_two) + epsilon)
    delta = (
        jnp.dot(old_basis, update.astype(jnp.bfloat16), preferred_element_type=jnp.float32)
        * inverse_root
    ).astype(jnp.bfloat16)

    sent = jnp.concatenate(
        [
            to_chunks(delta.reshape(owners, shard, quarter)),
            to_chunks(projected.astype(jnp.bfloat16))[:, None],
        ],
        axis=1,
    )
    sent, part = lax.optimization_barrier((sent, part))
    third_trip = exchange(sent)
    fresh = refresh(part, groups, root).reshape(owners, shard * rank_full // 1024, 8, 128)

    spread = pick(source, third_trip[:, pieces]).reshape(owners, capacity, 8, 128)
    sent = jnp.concatenate([spread, fresh], axis=1)
    back_delta = from_chunks(third_trip[:, :pieces], shard, quarter)
    sent, back_delta = lax.optimization_barrier((sent, back_delta))
    fourth_trip = exchange(sent)
    full_delta = gather_quarters(back_delta, groups, False, 2)
    new_weight = (weight.astype(jnp.float32) - step_size * full_delta.astype(jnp.float32)).astype(
        jnp.bfloat16
    )
    new_basis = from_chunks(fourth_trip[:, capacity:], shard, rank_full).astype(jnp.float32)
    spread = jnp.transpose(fourth_trip[:, :capacity], (1, 0, 2, 3))
    here_projected = from_chunks(spread, rank_full, quarter).astype(jnp.float32)
    matched = slots[:, None] == (here * capacity + jnp.arange(capacity, dtype=jnp.int32))[None, :]
    valid = jnp.any(matched, axis=0)[:, None, None]
    first_out = jnp.where(
        valid, beta_one * first_moment + (1.0 - beta_one) * here_projected, 0.0
    )
    second_out = jnp.where(
        valid,
        beta_two * second_moment + (1.0 - beta_two) * here_projected * here_projected,
        0.0,
    )

    return (new_weight, new_basis, first_out, second_out)


def solution(mesh):
    in_specs = (
        P("dp", None, "rows", None),
        P(None, "rows", None),
        P(None, "rows", None),
        P("rows", None, "dp"),
        P("rows", None, "dp"),
        P(),
        P(),
        P(),
    )
    out_specs = (
        P(None, "rows", None),
        P(None, "rows", None),
        P("rows", None, "dp"),
        P("rows", None, "dp"),
    )
    return jax.shard_map(
        per_device, mesh=mesh, in_specs=in_specs, out_specs=out_specs, check_vma=False
    )
```
